32 devices in a mesh: harm: 8 (over z, x), ax: 4 (over y, core).
Axes of the slice: x: 2, y: 2, z: 4, core: 2. Of those that a mesh axis runs over, the one named last changes fastest.
Arguments:
- forcing: bfloat16 [8, 4, 625, 256], P('harm', 'ax'), may hold values from -6 to 6
- jacobian: bfloat16 [8, 7, 4, 625, 625], P('harm', None, 'ax'), may hold values from -2 to 2
- lift_lower: bfloat16 [625, 125], replicated, may hold values from -0.15625 to 0.15625
- lift_upper: bfloat16 [625, 125], replicated, may hold values from -0.15625 to 0.15625
- orient: int32 [4], replicated, may hold values from 0 to 7
Outputs:
- solution: bfloat16 [8, 4, 625, 256], P('harm', 'ax')
The draws below stay inside these ranges and needn't reach their ends.
All inputs are finite; a program needn't handle non-finite values.
Results may differ from the reference program's by a relative error of at most 0.0041.
Values may be sent and summed in bfloat16 or wider, within the bound.
A program may use at most 64 MiB of HBM per device.

```python
import jax
import jax.numpy as jnp
from jax import lax

NVAR = 5
ND = 5
BAND = 7
ITERS = 3
COLS = 256
P_SIZE = 625
FN = 125
HARMONICS = 8
ELEMENTS = 4


def draw_jacobian(key, part):
    shape = (HARMONICS, BAND, ELEMENTS, P_SIZE, P_SIZE)
    spread = 0.3 * P_SIZE ** (-0.5)
    random_part = jax.random.normal(key, shape, jnp.float32) * spread
    random_part = jnp.clip(random_part, -6.0 * spread, 6.0 * spread)
    centre = (jnp.arange(BAND) == BAND // 2).astype(jnp.float32)[None, :, None, None, None]
    identity = jnp.eye(P_SIZE, dtype=jnp.float32)[None, None, None, :, :]
    return (random_part + centre * identity).astype(jnp.bfloat16)


def with_ends(array, own_key, least, largest):
    longest = array.shape.index(max(array.shape))
    spots = []
    for shift in (0, 1):
        where = [jax.random.randint(jax.random.fold_in(own_key, axis), (), 0, length) for axis, length in enumerate(array.shape)]
        where[longest] = (where[longest] + shift) % array.shape[longest]
        spots.append(tuple(where))
    return array.at[spots[0]].set(least).at[spots[1]].set(largest)


def block_scale(rng, extent, split, smallest, top_value):
    factor_of, own = 1.0, jax.random.fold_in(rng, 6)
    for axis_at, parts in split:
        draws = jnp.exp(jax.random.uniform(jax.random.fold_in(own, axis_at), (parts,), jnp.float32, smallest / len(split), top_value / len(split)))
        factor_of = factor_of * jnp.repeat(draws, extent[axis_at] // parts).reshape([-1 if axis == axis_at else 1 for axis in range(len(extent))])
    return factor_of


def scatter_about(own_key, extent, deviation, most, split=(), kind=jnp.bfloat16):
    level = block_scale(own_key, extent, split, -0.22, 0.18) if split else 1.0
    result = jax.random.normal(own_key, extent, jnp.float32) * deviation * level
    return jnp.minimum(jnp.maximum(result, -most), most).astype(kind)


def setup_inputs(seed: int = 0) -> dict:
    key_of = jax.random.split(jax.random.key(seed), 6)
    forcing = scatter_about(key_of[0], (HARMONICS, ELEMENTS, P_SIZE, COLS), 1.0, 6.0, ((0, 8), (1, 4)))
    jacobian = draw_jacobian(jax.random.fold_in(key_of[5], 71), 0)
    lift_lower = scatter_about(key_of[2], (P_SIZE, FN), (10 * FN) ** -0.5, 0.15625)
    lift_upper = scatter_about(key_of[3], (P_SIZE, FN), (10 * FN) ** -0.5, 0.15625)
    orient = with_ends(jax.random.randint(key_of[4], (ELEMENTS,), 0, 8), jax.random.fold_in(key_of[4], 1), 0, 7).astype(jnp.int32)
    return {"forcing": forcing, "jacobian": jacobian, "lift_lower": lift_lower, "lift_upper": lift_upper, "orient": orient}


relaxation = 0.5


def face_matrix(orient_value):
    positions = jnp.arange(ND * ND, dtype=jnp.int32)
    first_index = positions // ND
    second_index = positions % ND
    swapped = (orient_value // 4) % 2 == 1
    first_a = jnp.where(swapped, second_index, first_index)
    second_a = jnp.where(swapped, first_index, second_index)
    first_b = jnp.where(orient_value % 2 == 1, ND - 1 - first_a, first_a)
    second_b = jnp.where((orient_value // 2) % 2 == 1, ND - 1 - second_a, second_a)
    target = first_b * ND + second_b
    return (target[:, None] == positions[None, :]).astype(jnp.float32)


def apply_operator(iterate, jacobian, lift_lower, lift_upper, orient):
    harmonics = iterate.shape[0]
    elements = iterate.shape[1]
    columns = iterate.shape[3]
    reach = BAND // 2
    padded = jnp.pad(iterate, ((reach, reach), (0, 0), (0, 0), (0, 0)))

    def per_harmonic(inputs):
        blocks, harm_index = inputs
        window = lax.dynamic_slice_in_dim(padded, harm_index, BAND, 0)
        return jnp.einsum('jepq,jeqc->epc', blocks.astype(jnp.float32), window.astype(jnp.float32))

    coupled = lax.map(per_harmonic, (jacobian, jnp.arange(harmonics, dtype=jnp.int32)))
    shaped = iterate.reshape(harmonics, elements, NVAR, ND, ND * ND, columns)
    lower_trace = shaped[:, :, :, 0]
    upper_trace = shaped[:, :, :, ND - 1]
    lower_next = jnp.roll(lower_trace, -1, axis=1)
    upper_prev = jnp.roll(upper_trace, 1, axis=1)
    matrices = jax.vmap(face_matrix)(orient)
    matrices_prev = jnp.roll(matrices, 1, axis=0)
    upper_in = jnp.einsum('enm,hevmc->hevnc', matrices, lower_next.astype(jnp.float32))
    lower_in = jnp.einsum('enm,hevnc->hevmc', matrices_prev, upper_prev.astype(jnp.float32))
    upper_in = upper_in.reshape(harmonics, elements, FN, columns)
    lower_in = lower_in.reshape(harmonics, elements, FN, columns)
    face_term = jnp.einsum('pq,heqc->hepc', lift_upper.astype(jnp.float32), upper_in)
    face_term = face_term + jnp.einsum('pq,heqc->hepc', lift_lower.astype(jnp.float32), lower_in)
    return coupled + face_term


def reference(forcing, jacobian, lift_lower, lift_upper, orient):
    iterate = forcing
    for sweep in range(ITERS):
        applied = apply_operator(iterate, jacobian, lift_lower, lift_upper, orient)
        updated = iterate.astype(jnp.float32) + relaxation * (forcing.astype(jnp.float32) - applied)
        iterate = updated.astype(jnp.bfloat16)
    return iterate
```

```python
import functools

import jax
import jax.numpy as jnp
from jax import lax
from jax.experimental import pallas as pl
from jax.experimental.pallas import tpu as pltpu
from jax.sharding import PartitionSpec as P

NVAR = 5
ND = 5
BAND = 7
ITERS = 3
FN = 125
NF = ND * ND
NP = NVAR * ND * NF
FPAD = 128
PARTS = 2

relaxation = 0.5

A, B, C, D, E, F = range(6)
OFFSETS = (1, -2, 2, 3, -1, -3)
LOWER, UPPER = 6, 7
KINDS = 8
RELAYED = {A: 0, C: 1, E: 2}
PIECES = 5
ROW_TILE = 16


def divided(value, by):
    factor, shift = {5: (13108, 16), 25: (2622, 16), 125: (1049, 17)}[by]
    return lax.shift_right_logical(value * factor, shift)


def mapped(node, orient_value):
    swap = lax.rem(lax.div(orient_value, 4), 2)
    flip_b = lax.rem(orient_value, 2)
    flip_c = lax.rem(lax.div(orient_value, 2), 2)
    first = divided(node, ND)
    second = node - first * ND
    first_a = first + swap * (second - first)
    second_a = second + swap * (first - second)
    first_b = first_a + flip_b * (ND - 1 - 2 * first_a)
    second_b = second_a + flip_c * (ND - 1 - 2 * second_a)
    return first_b * ND + second_b


def kernel(
    harm_count, ax_count, width,
    orient_ref, forcing_ref, jac_ref, lower_ref, upper_ref, out_ref,
    jac, lift_lo, lift_up, own, slots, traces, faces, pick, acc,
    load_sem, jac_sem, send_sem, relay_sem, recv_sem,
):
    h = lax.axis_index("harm")
    e = lax.axis_index("ax")
    s = 1 - 2 * lax.rem(h, 2)
    reach = BAND // 2
    partner = h + s
    ahead = h + 2 * s
    behind = h - 2 * s
    has_ahead = jnp.logical_and(ahead >= 0, ahead < harm_count)
    has_behind = jnp.logical_and(behind >= 0, behind < harm_count)
    far = h - 3 * s
    has_far = jnp.logical_and(far >= 0, far < harm_count)
    has_both = jnp.logical_and(has_ahead, has_behind)
    above = lax.rem(e + 1, ax_count)
    below = lax.rem(e + ax_count - 1, ax_count)

    loads = [
        pltpu.make_async_copy(
            forcing_ref.at[0, 0, :, pl.ds(c * width, width)], own.at[0, c], load_sem.at[c]
        )
        for c in range(PARTS)
    ]
    for load in loads:
        load.start()
    jac_loads = [
        pltpu.make_async_copy(jac_ref.at[0, reach + k * s, 0], jac.at[i], jac_sem.at[i])
        for i, k in enumerate(OFFSETS + (0,))
    ]
    lift_loads = [
        pltpu.make_async_copy(lower_ref, lift_lo, load_sem.at[PARTS]),
        pltpu.make_async_copy(upper_ref, lift_up, load_sem.at[PARTS + 1]),
    ]
    for i in (BAND - 1, A, C, B, E, D, F):
        jac_loads[i].start()
    for load in lift_loads:
        load.start()

    barrier = pltpu.get_barrier_semaphore()

    def greet(axis, index):
        pl.semaphore_signal(
            barrier, inc=1, device_id={axis: index}, device_id_type=pl.DeviceIdType.MESH
        )

    greet("harm", partner)
    greet("ax", above)
    greet("ax", below)

    @pl.when(has_ahead)
    def _():
        greet("harm", ahead)

    @pl.when(has_behind)
    def _():
        greet("harm", behind)

    pl.semaphore_wait(
        barrier, 3 + has_ahead.astype(jnp.int32) + has_behind.astype(jnp.int32)
    )

    rows = own.shape[2]
    step = -(-rows // (PIECES * ROW_TILE)) * ROW_TILE
    cuts = [(start, min(step, rows - start)) for start in range(0, rows, step)]

    def transfer(t, c, kind, piece):
        mine = own.at[t, c]
        source, target = {
            A: (mine, partner),
            B: (mine, ahead),
            C: (mine, behind),
            D: (slots.at[A, t, c], behind),
            E: (slots.at[C, t, c], partner),
            F: (slots.at[E, t, c], ahead),
        }[kind]
        part = slice(None) if piece is None else pl.ds(*cuts[piece])
        return pltpu.make_async_remote_copy(
            src_ref=source.at[part],
            dst_ref=slots.at[kind, t, c, part],
            send_sem=send_sem.at[kind],
            recv_sem=relay_sem.at[t, c, RELAYED[kind], piece]
            if kind in RELAYED
            else recv_sem.at[t, c, kind],
            device_id={"harm": target},
            device_id_type=pl.DeviceIdType.MESH,
        )

    sending = {
        A: None, B: has_ahead, C: has_behind, D: has_behind, E: has_ahead, F: has_both
    }
    getting = {
        A: None, B: has_behind, C: has_ahead, D: has_ahead, E: has_behind, F: has_far
    }

    def guarded(condition, action):
        if condition is None:
            action()
        else:
            pl.when(condition)(action)

    def face_transfers(t, c):
        result = []
        for place, kind, target in ((0, LOWER, below), (1, UPPER, above)):
            result.append(
                pltpu.make_async_remote_copy(
                    src_ref=traces.at[place, t, c],
                    dst_ref=faces.at[place, t, c],
                    send_sem=send_sem.at[kind],
                    recv_sem=recv_sem.at[t, c, kind],
                    device_id={"ax": target},
                    device_id_type=pl.DeviceIdType.MESH,
                )
            )
        return result

    def send_own(t, c, kinds):
        for piece in range(len(cuts)):
            send_piece(t, c, piece, kinds)

    def send_piece(t, c, piece, kinds=(C, A)):
        for kind in kinds:
            guarded(sending[kind], lambda: transfer(t, c, kind, piece).start())

    def send_late(t, c):
        guarded(sending[B], lambda: transfer(t, c, B, None).start())

    def send_traces(t, c):
        for place in range(2):
            traces[place, t, c] = jnp.dot(
                pick[place], own[t, c], preferred_element_type=jnp.float32
            ).astype(jnp.bfloat16)
        for copy in face_transfers(t, c):
            copy.start()

    def add(t, c, kind, wait=False):
        def action():
            if wait:
                transfer(t, c, kind, None).wait_recv()
            acc[c] += jnp.dot(jac[kind], slots[kind, t, c], preferred_element_type=jnp.float32)

        guarded(getting[kind], action)

    def begin(t, c):
        acc[c] = jnp.dot(jac[BAND - 1], own[t, c], preferred_element_type=jnp.float32)

    loads[0].wait()
    send_own(0, 0, (C, A))
    send_late(0, 0)
    loads[1].wait()
    send_own(0, 1, (C,))

    row = lax.broadcasted_iota(jnp.int32, (FPAD, NP), 0)
    column = lax.broadcasted_iota(jnp.int32, (FPAD, NP), 1)
    row_variable = divided(row, NF)
    row_node = row - row_variable * NF
    column_variable = divided(column, FN)
    column_node = column - column_variable * FN
    low_target = row_variable * FN + mapped(row_node, orient_ref[below])
    pick[0] = jnp.where(column == low_target, 1.0, 0.0).astype(jnp.bfloat16)
    up_node = column_node - (ND - 1) * NF
    up_image = mapped(jnp.maximum(up_node, 0), orient_ref[e])
    up_row = jnp.where(up_node >= 0, column_variable * NF + up_image, -1)
    pick[1] = jnp.where(up_row == row, 1.0, 0.0).astype(jnp.bfloat16)

    send_traces(0, 0)

    def gather(t, c, tasks=()):
        tasks = list(tasks)
        count = len(cuts)
        for piece in range(count):

            def from_ahead(piece=piece):
                transfer(t, c, C, piece).wait_recv()
                transfer(t, c, E, piece).start()

            pl.when(has_ahead)(from_ahead)
            transfer(t, c, A, piece).wait_recv()
            pl.when(has_behind)(lambda: transfer(t, c, D, piece).start())
            for task in tasks[piece : piece + 1] if piece < count - 1 else tasks[piece:]:
                task()

    def pass_on(t, c, tasks=()):
        tasks = list(tasks)
        count = len(cuts)
        for piece in range(count):

            def onward(piece=piece):
                transfer(t, c, E, piece).wait_recv()
                pl.when(has_ahead)(lambda: transfer(t, c, F, piece).start())

            pl.when(has_behind)(onward)
            for task in tasks[piece : piece + 1] if piece < count - 1 else tasks[piece:]:
                task()

    def add_faces(t, c):
        for copy in face_transfers(t, c):
            copy.wait_recv()
        acc[c] += jnp.dot(
            lift_up[...], faces[0, t, c, :FN], preferred_element_type=jnp.float32
        ) + jnp.dot(lift_lo[...], faces[1, t, c, :FN], preferred_element_type=jnp.float32)

    def finish(t, c, send):
        guarded(getting[F], lambda: transfer(t, c, F, None).wait_recv())
        for piece, (start, size) in enumerate(cuts):
            part = slice(start, start + size)

            def update(last_term):
                total = acc[c, part]
                if last_term:
                    total = total + jnp.dot(
                        jac[F, part], slots[F, t, c], preferred_element_type=jnp.float32
                    )
                updated = own[t, c, part].astype(jnp.float32) + relaxation * (
                    own[0, c, part].astype(jnp.float32) - total
                )
                updated = updated.astype(jnp.bfloat16)
                if send is None:
                    out_ref[0, 0, part, c * width : (c + 1) * width] = updated
                else:
                    own[t + 1, c, part] = updated

            pl.when(has_far)(lambda: update(True))
            pl.when(jnp.logical_not(has_far))(lambda: update(False))
            if send is True:
                send_piece(t + 1, c, piece)
            elif send is not None:
                pl.when(send)(lambda: send_piece(t + 1, c, piece))

    def steps(t, c):
        return [
            lambda: add(t, c, E),
            lambda: add(t, c, B, wait=True),
            lambda: add(t, c, D, wait=True),
            lambda: add_faces(t, c),
        ]

    def sweep(t, carry):
        first = t == 0
        last = t == ITERS - 1
        again = jnp.logical_not(first)
        more = jnp.logical_not(last)

        def opening():
            gather(0, 0)
            send_own(0, 1, (A,))

        def earlier():
            before = steps(t - 1, 1)
            before[0]()
            gather(t, 0, [lambda: send_traces(t, 0)] + before[1:])
            finish(t - 1, 1, True)

        pl.when(first)(opening)
        pl.when(again)(earlier)

        @pl.when(first)
        def _():
            for index in range(BAND):
                jac_loads[index].wait()
            for load in lift_loads:
                load.wait()

        pass_on(t, 0, [lambda: begin(t, 0), lambda: add(t, 0, A), lambda: add(t, 0, C)])
        send_late(t, 1)
        middle = steps(t, 0)
        middle[0]()
        gather(t, 1, [lambda: send_traces(t, 1)] + middle[1:])
        finish(t, 0, more)
        pass_on(t, 1, [lambda: begin(t, 1), lambda: add(t, 1, A), lambda: add(t, 1, C)])
        pl.when(more)(lambda: send_late(t + 1, 0))
        return carry

    lax.fori_loop(0, ITERS, sweep, 0)
    store = pltpu.make_async_copy(
        own.at[ITERS, 0], out_ref.at[0, 0, :, pl.ds(0, width)], load_sem.at[0]
    )
    store.start()
    for task in steps(ITERS - 1, 1):
        task()
    for kind, condition in sending.items():

        def wait(kind=kind):
            pltpu.make_async_remote_copy(
                src_ref=slots.at[kind],
                dst_ref=slots.at[kind],
                send_sem=send_sem.at[kind],
                recv_sem=recv_sem.at[0, 0, 0],
                device_id={"harm": partner},
                device_id_type=pl.DeviceIdType.MESH,
            ).wait_send()

        guarded(condition, wait)
    for place, kind, target in ((0, LOWER, below), (1, UPPER, above)):
        pltpu.make_async_remote_copy(
            src_ref=traces.at[place],
            dst_ref=faces.at[place],
            send_sem=send_sem.at[kind],
            recv_sem=recv_sem.at[0, 0, kind],
            device_id={"ax": target},
            device_id_type=pl.DeviceIdType.MESH,
        ).wait_send()
    finish(ITERS - 1, 1, None)
    store.wait()


def local(forcing, jacobian, lift_lower, lift_upper, orient):
    rows, columns = forcing.shape[2:]
    width = columns // PARTS
    bf16 = jnp.bfloat16
    any_space = pl.BlockSpec(memory_space=pl.ANY)
    return pl.pallas_call(
        functools.partial(kernel, lax.axis_size("harm"), lax.axis_size("ax"), width),
        out_shape=pltpu.VMEM(forcing.shape, bf16),
        in_specs=[pl.BlockSpec(memory_space=pltpu.SMEM)] + [any_space] * 4,
        out_specs=pl.BlockSpec(memory_space=pltpu.VMEM),
        scratch_shapes=[
            pltpu.VMEM((BAND, rows, rows), bf16),
            pltpu.VMEM(lift_lower.shape, bf16),
            pltpu.VMEM(lift_upper.shape, bf16),
            pltpu.VMEM((ITERS + 1, PARTS, rows, width), bf16),
            pltpu.VMEM((6, ITERS, PARTS, rows, width), bf16),
            pltpu.VMEM((2, ITERS, PARTS, FPAD, width), bf16),
            pltpu.VMEM((2, ITERS, PARTS, FPAD, width), bf16),
            pltpu.VMEM((2, FPAD, rows), bf16),
            pltpu.VMEM((PARTS, rows, width), jnp.float32),
            pltpu.SemaphoreType.DMA((PARTS + 2,)),
            pltpu.SemaphoreType.DMA((BAND,)),
            pltpu.SemaphoreType.DMA((KINDS,)),
            pltpu.SemaphoreType.DMA((ITERS, PARTS, len(RELAYED), PIECES)),
            pltpu.SemaphoreType.DMA((ITERS, PARTS, KINDS)),
        ],
        compiler_params=pltpu.CompilerParams(collective_id=0, has_side_effects=True),
        name="sweeps",
    )(orient, forcing, jacobian, lift_lower, lift_upper)


def solution(mesh):
    placed = (P("harm", "ax", None, None), P("harm", None, "ax", None, None), P(), P(), P())
    return jax.shard_map(
        local, mesh=mesh, in_specs=placed, out_specs=P("harm", "ax", None, None), check_vma=False
    )
```

```python
import functools

import jax
import jax.numpy as jnp
from jax import lax
from jax.experimental import pallas as pl
from jax.experimental.pallas import tpu as pltpu
from jax.sharding import PartitionSpec as P

NVAR = 5
ND = 5
BAND = 7
ITERS = 3
FN = 125
NF = ND * ND
NP = NVAR * ND * NF
FPAD = 128
PARTS = 2

relaxation = 0.5

A, B, C, D, E, F = range(6)
OFFSETS = (1, -2, 2, 3, -1, -3)
LOWER, UPPER = 6, 7
KINDS = 8
RELAYED = {A: 0, C: 1, E: 2}
PIECES = 4
DIRECT = (3,)
ROW_TILE = 16


def divided(value, by):
    factor, shift = {5: (13108, 16), 25: (2622, 16), 125: (1049, 17)}[by]
    return lax.shift_right_logical(value * factor, shift)


def mapped(node, orient_value):
    swap = lax.rem(lax.div(orient_value, 4), 2)
    flip_b = lax.rem(orient_value, 2)
    flip_c = lax.rem(lax.div(orient_value, 2), 2)
    first = divided(node, ND)
    second = node - first * ND
    first_a = first + swap * (second - first)
    second_a = second + swap * (first - second)
    first_b = first_a + flip_b * (ND - 1 - 2 * first_a)
    second_b = second_a + flip_c * (ND - 1 - 2 * second_a)
    return first_b * ND + second_b


def kernel(
    harm_count, ax_count, width,
    orient_ref, forcing_ref, jac_ref, lower_ref, upper_ref, out_ref,
    jac, lift_lo, lift_up, own, slots, traces, faces, pick, acc,
    load_sem, jac_sem, send_sem, relay_sem, recv_sem,
):
    h = lax.axis_index("harm")
    e = lax.axis_index("ax")
    s = 1 - 2 * lax.rem(h, 2)
    reach = BAND // 2
    partner = h + s
    ahead = h + 2 * s
    behind = h - 2 * s
    has_ahead = jnp.logical_and(ahead >= 0, ahead < harm_count)
    has_behind = jnp.logical_and(behind >= 0, behind < harm_count)
    far = h - 3 * s
    has_far = jnp.logical_and(far >= 0, far < harm_count)
    has_both = jnp.logical_and(has_ahead, has_behind)
    above = lax.rem(e + 1, ax_count)
    below = lax.rem(e + ax_count - 1, ax_count)

    barrier = pltpu.get_barrier_semaphore()

    across = h - s
    has_across = jnp.logical_and(across >= 0, across < harm_count)

    def greet(axis, index):
        pl.semaphore_signal(
            barrier, inc=1, device_id={axis: index}, device_id_type=pl.DeviceIdType.MESH
        )

    greet("harm", partner)
    greet("ax", above)
    greet("ax", below)

    @pl.when(has_ahead)
    def _():
        greet("harm", ahead)

    @pl.when(has_behind)
    def _():
        greet("harm", behind)

    @pl.when(has_across)
    def _():
        greet("harm", across)

    loads = [
        pltpu.make_async_copy(
            forcing_ref.at[0, 0, :, pl.ds(c * width, width)], own.at[0, c], load_sem.at[c]
        )
        for c in range(PARTS)
    ]
    for load in loads:
        load.start()
    jac_loads = [
        pltpu.make_async_copy(jac_ref.at[0, reach + k * s, 0], jac.at[i], jac_sem.at[i])
        for i, k in enumerate(OFFSETS + (0,))
    ]
    lift_loads = [
        pltpu.make_async_copy(lower_ref, lift_lo, load_sem.at[PARTS]),
        pltpu.make_async_copy(upper_ref, lift_up, load_sem.at[PARTS + 1]),
    ]

    pl.semaphore_wait(
        barrier,
        3
        + has_ahead.astype(jnp.int32)
        + has_behind.astype(jnp.int32)
        + has_across.astype(jnp.int32),
    )

    rows = own.shape[2]
    step = -(-rows // (PIECES * ROW_TILE)) * ROW_TILE
    cuts = [(start, min(step, rows - start)) for start in range(0, rows, step)]

    def transfer(t, c, kind, piece, direct=False):
        mine = own.at[t, c]
        source, target = {
            A: (mine, partner),
            B: (mine, ahead),
            C: (mine, behind),
            D: (slots.at[A, t, c], behind),
            E: (slots.at[C, t, c], partner),
            F: (slots.at[C, t, c], across) if direct else (slots.at[E, t, c], ahead),
        }[kind]
        part = slice(None) if piece is None else pl.ds(*cuts[piece])
        return pltpu.make_async_remote_copy(
            src_ref=source.at[part],
            dst_ref=slots.at[kind, t, c, part],
            send_sem=send_sem.at[kind],
            recv_sem=relay_sem.at[t, c, RELAYED[kind], piece]
            if kind in RELAYED
            else recv_sem.at[t, c, kind],
            device_id={"harm": target},
            device_id_type=pl.DeviceIdType.MESH,
        )

    sending = {
        A: None, B: has_ahead, C: has_behind, D: has_behind, E: has_ahead, F: has_both
    }
    getting = {
        A: None, B: has_behind, C: has_ahead, D: has_ahead, E: has_behind, F: has_far
    }

    def guarded(condition, action):
        if condition is None:
            action()
        else:
            pl.when(condition)(action)

    def face_transfers(t, c):
        result = []
        for place, kind, target in ((0, LOWER, below), (1, UPPER, above)):
            result.append(
                pltpu.make_async_remote_copy(
                    src_ref=traces.at[place, t, c],
                    dst_ref=faces.at[place, t, c],
                    send_sem=send_sem.at[kind],
                    recv_sem=recv_sem.at[t, c, kind],
                    device_id={"ax": target},
                    device_id_type=pl.DeviceIdType.MESH,
                )
            )
        return result

    def send_own(t, c, kinds):
        for piece in range(len(cuts)):
            send_piece(t, c, piece, kinds)

    def send_piece(t, c, piece, kinds=(C, A)):
        for kind in kinds:
            guarded(sending[kind], lambda: transfer(t, c, kind, piece).start())

    def send_late(t, c):
        guarded(sending[B], lambda: transfer(t, c, B, None).start())

    def send_traces(t, c):
        for place in range(2):
            traces[place, t, c] = jnp.dot(
                pick[place], own[t, c], preferred_element_type=jnp.float32
            ).astype(jnp.bfloat16)
        for copy in face_transfers(t, c):
            copy.start()

    def add(t, c, kind, wait=False):
        def action():
            if wait:
                transfer(t, c, kind, None).wait_recv()
            acc[c] += jnp.dot(jac[kind], slots[kind, t, c], preferred_element_type=jnp.float32)

        guarded(getting[kind], action)

    def begin(t, c):
        acc[c] = jnp.dot(jac[BAND - 1], own[t, c], preferred_element_type=jnp.float32)

    loads[0].wait()
    send_own(0, 0, (C, A))
    send_late(0, 0)
    loads[1].wait()
    send_own(0, 1, (C,))
    for i in (BAND - 1, A, C, B, E, D, F):
        jac_loads[i].start()
    for load in lift_loads:
        load.start()

    row = lax.broadcasted_iota(jnp.int32, (FPAD, NP), 0)
    column = lax.broadcasted_iota(jnp.int32, (FPAD, NP), 1)
    row_variable = divided(row, NF)
    row_node = row - row_variable * NF
    column_variable = divided(column, FN)
    column_node = column - column_variable * FN
    low_target = row_variable * FN + mapped(row_node, orient_ref[below])
    pick[0] = jnp.where(column == low_target, 1.0, 0.0).astype(jnp.bfloat16)
    up_node = column_node - (ND - 1) * NF
    up_image = mapped(jnp.maximum(up_node, 0), orient_ref[e])
    up_row = jnp.where(up_node >= 0, column_variable * NF + up_image, -1)
    pick[1] = jnp.where(up_row == row, 1.0, 0.0).astype(jnp.bfloat16)

    send_traces(0, 0)

    def gather(t, c, tasks=(), straight=None):
        tasks = list(tasks)
        count = len(cuts)
        for piece in range(count):

            def from_ahead(piece=piece):
                transfer(t, c, C, piece).wait_recv()
                if straight is not None and piece in DIRECT:
                    pl.when(jnp.logical_and(straight, has_across))(
                        lambda: transfer(t, c, F, piece, True).start()
                    )
                transfer(t, c, E, piece).start()

            pl.when(has_ahead)(from_ahead)
            transfer(t, c, A, piece).wait_recv()
            pl.when(has_behind)(lambda: transfer(t, c, D, piece).start())
            for task in tasks[piece : piece + 1] if piece < count - 1 else tasks[piece:]:
                task()

    def pass_on(t, c, tasks=(), straight=None):
        tasks = list(tasks)
        count = len(cuts)
        for piece in range(count):

            def onward(piece=piece):
                transfer(t, c, E, piece).wait_recv()
                onward_too = has_ahead
                if straight is not None and piece in DIRECT:
                    onward_too = jnp.logical_and(has_ahead, jnp.logical_not(straight))
                pl.when(onward_too)(lambda: transfer(t, c, F, piece).start())

            pl.when(has_behind)(onward)
            for task in tasks[piece : piece + 1] if piece < count - 1 else tasks[piece:]:
                task()

    def add_faces(t, c):
        for copy in face_transfers(t, c):
            copy.wait_recv()
        acc[c] += jnp.dot(
            lift_up[...], faces[0, t, c, :FN], preferred_element_type=jnp.float32
        ) + jnp.dot(lift_lo[...], faces[1, t, c, :FN], preferred_element_type=jnp.float32)

    def finish(t, c, send):
        guarded(getting[F], lambda: transfer(t, c, F, None).wait_recv())
        for piece, (start, size) in enumerate(cuts):
            part = slice(start, start + size)

            def update(last_term):
                total = acc[c, part]
                if last_term:
                    total = total + jnp.dot(
                        jac[F, part], slots[F, t, c], preferred_element_type=jnp.float32
                    )
                updated = own[t, c, part].astype(jnp.float32) + relaxation * (
                    own[0, c, part].astype(jnp.float32) - total
                )
                updated = updated.astype(jnp.bfloat16)
                if send is None:
                    out_ref[0, 0, part, c * width : (c + 1) * width] = updated
                else:
                    own[t + 1, c, part] = updated

            pl.when(has_far)(lambda: update(True))
            pl.when(jnp.logical_not(has_far))(lambda: update(False))
            if send:
                send_piece(t + 1, c, piece)

    def steps(t, c):
        return [
            lambda: add(t, c, E),
            lambda: add(t, c, B, wait=True),
            lambda: add(t, c, D, wait=True),
            lambda: add_faces(t, c),
        ]

    def sweep(t):
        first = t == 0
        last = t == ITERS - 1
        more = not last
        straight = lax.rem(e, 2) == 0 if last else None

        def opening():
            gather(0, 0)
            send_own(0, 1, (A,))

        def earlier():
            before = steps(t - 1, 1)
            before[0]()
            gather(t, 0, [lambda: send_traces(t, 0)] + [lambda: None] + before[1:2] + before[2:3] + before[3:4])
            finish(t - 1, 1, True)

        opening() if first else earlier()

        if first:
            for index in range(BAND):
                jac_loads[index].wait()
            for load in lift_loads:
                load.wait()

        pass_on(t, 0, [lambda: begin(t, 0), lambda: add(t, 0, A), lambda: add(t, 0, C)])
        send_late(t, 1)
        middle = steps(t, 0)
        middle[0]()
        gather(t, 1, [lambda: send_traces(t, 1)] + [lambda: None] + middle[1:2] + middle[2:3] + middle[3:4], straight)
        finish(t, 0, more)
        pass_on(
            t, 1, [lambda: begin(t, 1), lambda: add(t, 1, A), lambda: add(t, 1, C)], straight
        )
        if more:
            send_late(t + 1, 0)

    for t in range(ITERS):
        sweep(t)
    store = pltpu.make_async_copy(
        own.at[ITERS, 0], out_ref.at[0, 0, :, pl.ds(0, width)], load_sem.at[0]
    )
    store.start()
    for task in steps(ITERS - 1, 1):
        task()
    for kind, condition in sending.items():

        def wait(kind=kind):
            pltpu.make_async_remote_copy(
                src_ref=slots.at[kind],
                dst_ref=slots.at[kind],
                send_sem=send_sem.at[kind],
                recv_sem=recv_sem.at[0, 0, 0],
                device_id={"harm": partner},
                device_id_type=pl.DeviceIdType.MESH,
            ).wait_send()

        guarded(condition, wait)
    for place, kind, target in ((0, LOWER, below), (1, UPPER, above)):
        pltpu.make_async_remote_copy(
            src_ref=traces.at[place],
            dst_ref=faces.at[place],
            send_sem=send_sem.at[kind],
            recv_sem=recv_sem.at[0, 0, kind],
            device_id={"ax": target},
            device_id_type=pl.DeviceIdType.MESH,
        ).wait_send()
    finish(ITERS - 1, 1, None)
    store.wait()


def local(forcing, jacobian, lift_lower, lift_upper, orient):
    rows, columns = forcing.shape[2:]
    width = columns // PARTS
    bf16 = jnp.bfloat16
    any_space = pl.BlockSpec(memory_space=pl.ANY)
    return pl.pallas_call(
        functools.partial(kernel, lax.axis_size("harm"), lax.axis_size("ax"), width),
        out_shape=pltpu.VMEM(forcing.shape, bf16),
        in_specs=[pl.BlockSpec(memory_space=pltpu.SMEM)] + [any_space] * 4,
        out_specs=pl.BlockSpec(memory_space=pltpu.VMEM),
        scratch_shapes=[
            pltpu.VMEM((BAND, rows, rows), bf16),
            pltpu.VMEM(lift_lower.shape, bf16),
            pltpu.VMEM(lift_upper.shape, bf16),
            pltpu.VMEM((ITERS + 1, PARTS, rows, width), bf16),
            pltpu.VMEM((6, ITERS, PARTS, rows, width), bf16),
            pltpu.VMEM((2, ITERS, PARTS, FPAD, width), bf16),
            pltpu.VMEM((2, ITERS, PARTS, FPAD, width), bf16),
            pltpu.VMEM((2, FPAD, rows), bf16),
            pltpu.VMEM((PARTS, rows, width), jnp.float32),
            pltpu.SemaphoreType.DMA((PARTS + 2,)),
            pltpu.SemaphoreType.DMA((BAND,)),
            pltpu.SemaphoreType.DMA((KINDS,)),
            pltpu.SemaphoreType.DMA((ITERS, PARTS, len(RELAYED), PIECES)),
            pltpu.SemaphoreType.DMA((ITERS, PARTS, KINDS)),
        ],
        compiler_params=pltpu.CompilerParams(collective_id=0, has_side_effects=True),
        name="sweeps",
    )(orient, forcing, jacobian, lift_lower, lift_upper)


def solution(mesh):
    placed = (P("harm", "ax", None, None), P("harm", None, "ax", None, None), P(), P(), P())
    return jax.shard_map(
        local, mesh=mesh, in_specs=placed, out_specs=P("harm", "ax", None, None), check_vma=False
    )
```

```python
import functools

import jax
import jax.numpy as jnp
from jax import lax
from jax.experimental import pallas as pl
from jax.experimental.pallas import tpu as pltpu
from jax.sharding import PartitionSpec as P

NVAR = 5
ND = 5
BAND = 7
ITERS = 3
FN = 125
NF = ND * ND
NP = NVAR * ND * NF
FPAD = 128
PARTS = 2

relaxation = 0.5

A, B, C, D, E, F = range(6)
OFFSETS = (1, -2, 2, 3, -1, -3)
LOWER, UPPER = 6, 7
KINDS = 8
RELAYED = {A: 0, C: 1, E: 2}
PIECES = 4
DIRECT = (3,)
ROW_TILE = 16


def divided(value, by):
    factor, shift = {5: (13108, 16), 25: (2622, 16), 125: (1049, 17)}[by]
    return lax.shift_right_logical(value * factor, shift)


def mapped(node, orient_value):
    swap = lax.rem(lax.div(orient_value, 4), 2)
    flip_b = lax.rem(orient_value, 2)
    flip_c = lax.rem(lax.div(orient_value, 2), 2)
    first = divided(node, ND)
    second = node - first * ND
    first_a = first + swap * (second - first)
    second_a = second + swap * (first - second)
    first_b = first_a + flip_b * (ND - 1 - 2 * first_a)
    second_b = second_a + flip_c * (ND - 1 - 2 * second_a)
    return first_b * ND + second_b


def kernel(
    harm_count, ax_count, width,
    orient_ref, forcing_ref, jac_ref, lower_ref, upper_ref, out_ref,
    jac, lift_lo, lift_up, own, slots, traces, faces, pick, acc,
    load_sem, jac_sem, send_sem, relay_sem, recv_sem,
):
    h = lax.axis_index("harm")
    e = lax.axis_index("ax")
    s = 1 - 2 * lax.rem(h, 2)
    reach = BAND // 2
    partner = h + s
    ahead = h + 2 * s
    behind = h - 2 * s
    has_ahead = jnp.logical_and(ahead >= 0, ahead < harm_count)
    has_behind = jnp.logical_and(behind >= 0, behind < harm_count)
    far = h - 3 * s
    has_far = jnp.logical_and(far >= 0, far < harm_count)
    has_both = jnp.logical_and(has_ahead, has_behind)
    above = lax.rem(e + 1, ax_count)
    below = lax.rem(e + ax_count - 1, ax_count)

    barrier = pltpu.get_barrier_semaphore()

    across = h - s
    has_across = jnp.logical_and(across >= 0, across < harm_count)

    def greet(axis, index):
        pl.semaphore_signal(
            barrier, inc=1, device_id={axis: index}, device_id_type=pl.DeviceIdType.MESH
        )

    greet("harm", partner)
    greet("ax", above)
    greet("ax", below)

    @pl.when(has_ahead)
    def _():
        greet("harm", ahead)

    @pl.when(has_behind)
    def _():
        greet("harm", behind)

    @pl.when(has_across)
    def _():
        greet("harm", across)

    loads = [
        pltpu.make_async_copy(
            forcing_ref.at[0, 0, :, pl.ds(c * width, width)], own.at[0, c], load_sem.at[c]
        )
        for c in range(PARTS)
    ]
    for load in loads:
        load.start()
    jac_loads = [
        pltpu.make_async_copy(jac_ref.at[0, reach + k * s, 0], jac.at[i], jac_sem.at[i])
        for i, k in enumerate(OFFSETS + (0,))
    ]
    lift_loads = [
        pltpu.make_async_copy(lower_ref, lift_lo, load_sem.at[PARTS]),
        pltpu.make_async_copy(upper_ref, lift_up, load_sem.at[PARTS + 1]),
    ]

    pl.semaphore_wait(
        barrier,
        3
        + has_ahead.astype(jnp.int32)
        + has_behind.astype(jnp.int32)
        + has_across.astype(jnp.int32),
    )

    rows = own.shape[2]
    step = -(-rows // (PIECES * ROW_TILE)) * ROW_TILE
    cuts = [(start, min(step, rows - start)) for start in range(0, rows, step)]

    def transfer(t, c, kind, piece, direct=False):
        mine = own.at[t, c]
        source, target = {
            A: (mine, partner),
            B: (mine, ahead),
            C: (mine, behind),
            D: (slots.at[A, t, c], behind),
            E: (slots.at[C, t, c], partner),
            F: (slots.at[C, t, c], across) if direct else (slots.at[E, t, c], ahead),
        }[kind]
        part = slice(None) if piece is None else pl.ds(*cuts[piece])
        return pltpu.make_async_remote_copy(
            src_ref=source.at[part],
            dst_ref=slots.at[kind, t, c, part],
            send_sem=send_sem.at[kind],
            recv_sem=relay_sem.at[t, c, RELAYED[kind], piece]
            if kind in RELAYED
            else recv_sem.at[t, c, kind],
            device_id={"harm": target},
            device_id_type=pl.DeviceIdType.MESH,
        )

    sending = {
        A: None, B: has_ahead, C: has_behind, D: has_behind, E: has_ahead, F: has_both
    }
    getting = {
        A: None, B: has_behind, C: has_ahead, D: has_ahead, E: has_behind, F: has_far
    }

    def guarded(condition, action):
        if condition is None:
            action()
        else:
            pl.when(condition)(action)

    def face_transfers(t, c):
        result = []
        for place, kind, target in ((0, LOWER, below), (1, UPPER, above)):
            result.append(
                pltpu.make_async_remote_copy(
                    src_ref=traces.at[place, t, c],
                    dst_ref=faces.at[place, t, c],
                    send_sem=send_sem.at[kind],
                    recv_sem=recv_sem.at[t, c, kind],
                    device_id={"ax": target},
                    device_id_type=pl.DeviceIdType.MESH,
                )
            )
        return result

    def send_own(t, c, kinds):
        for piece in range(len(cuts)):
            send_piece(t, c, piece, kinds)

    def send_piece(t, c, piece, kinds=(C, A)):
        for kind in kinds:
            guarded(sending[kind], lambda: transfer(t, c, kind, piece).start())

    def send_late(t, c):
        guarded(sending[B], lambda: transfer(t, c, B, None).start())

    def send_traces(t, c):
        for place in range(2):
            traces[place, t, c] = jnp.dot(
                pick[place], own[t, c], preferred_element_type=jnp.float32
            ).astype(jnp.bfloat16)
        for copy in face_transfers(t, c):
            copy.start()

    def add(t, c, kind, wait=False):
        def action():
            if wait:
                transfer(t, c, kind, None).wait_recv()
            acc[c] += jnp.dot(jac[kind], slots[kind, t, c], preferred_element_type=jnp.float32)

        guarded(getting[kind], action)

    def begin(t, c):
        acc[c] = jnp.dot(jac[BAND - 1], own[t, c], preferred_element_type=jnp.float32)

    loads[0].wait()
    send_own(0, 0, (C, A))
    send_late(0, 0)
    loads[1].wait()
    send_own(0, 1, (C,))
    for i in (BAND - 1, A, C, B, E, D, F):
        jac_loads[i].start()
    for load in lift_loads:
        load.start()

    row = lax.broadcasted_iota(jnp.int32, (FPAD, NP), 0)
    column = lax.broadcasted_iota(jnp.int32, (FPAD, NP), 1)
    row_variable = divided(row, NF)
    row_node = row - row_variable * NF
    column_variable = divided(column, FN)
    column_node = column - column_variable * FN
    low_target = row_variable * FN + mapped(row_node, orient_ref[below])
    pick[0] = jnp.where(column == low_target, 1.0, 0.0).astype(jnp.bfloat16)
    up_node = column_node - (ND - 1) * NF
    up_image = mapped(jnp.maximum(up_node, 0), orient_ref[e])
    up_row = jnp.where(up_node >= 0, column_variable * NF + up_image, -1)
    pick[1] = jnp.where(up_row == row, 1.0, 0.0).astype(jnp.bfloat16)

    send_traces(0, 0)

    def gather(t, c, tasks=(), straight=None):
        tasks = list(tasks)
        count = len(cuts)
        for piece in range(count):

            def from_ahead(piece=piece):
                transfer(t, c, C, piece).wait_recv()
                if straight is not None and piece in DIRECT:
                    pl.when(jnp.logical_and(straight, has_across))(
                        lambda: transfer(t, c, F, piece, True).start()
                    )
                transfer(t, c, E, piece).start()

            pl.when(has_ahead)(from_ahead)
            transfer(t, c, A, piece).wait_recv()
            pl.when(has_behind)(lambda: transfer(t, c, D, piece).start())
            for task in tasks[piece : piece + 1] if piece < count - 1 else tasks[piece:]:
                task()

    def pass_on(t, c, tasks=(), straight=None):
        tasks = list(tasks)
        count = len(cuts)
        for piece in range(count):

            def onward(piece=piece):
                transfer(t, c, E, piece).wait_recv()
                onward_too = has_ahead
                if straight is not None and piece in DIRECT:
                    onward_too = jnp.logical_and(has_ahead, jnp.logical_not(straight))
                pl.when(onward_too)(lambda: transfer(t, c, F, piece).start())

            pl.when(has_behind)(onward)
            for task in tasks[piece : piece + 1] if piece < count - 1 else tasks[piece:]:
                task()

    def add_faces(t, c):
        for copy in face_transfers(t, c):
            copy.wait_recv()
        acc[c] += jnp.dot(
            lift_up[...], faces[0, t, c, :FN], preferred_element_type=jnp.float32
        ) + jnp.dot(lift_lo[...], faces[1, t, c, :FN], preferred_element_type=jnp.float32)

    def finish(t, c, send):
        merged = send is not None
        if merged:
            guarded(getting[D], lambda: transfer(t, c, D, None).wait_recv())
        guarded(getting[F], lambda: transfer(t, c, F, None).wait_recv())
        for piece, (start, size) in enumerate(cuts):
            part = slice(start, start + size)

            def update(last_term, far_term):
                total = acc[c, part]
                if far_term:
                    total = total + jnp.dot(
                        jac[D, part], slots[D, t, c], preferred_element_type=jnp.float32
                    )
                if last_term:
                    total = total + jnp.dot(
                        jac[F, part], slots[F, t, c], preferred_element_type=jnp.float32
                    )
                updated = own[t, c, part].astype(jnp.float32) + relaxation * (
                    own[0, c, part].astype(jnp.float32) - total
                )
                updated = updated.astype(jnp.bfloat16)
                if send is None:
                    out_ref[0, 0, part, c * width : (c + 1) * width] = updated
                else:
                    own[t + 1, c, part] = updated

            if merged:
                short = jnp.logical_and(has_ahead, jnp.logical_not(has_far))
                pl.when(jnp.logical_and(has_ahead, has_far))(lambda: update(True, True))
                pl.when(short)(lambda: update(False, True))
                alone = jnp.logical_not(has_ahead)
                pl.when(jnp.logical_and(alone, has_far))(lambda: update(True, False))
                pl.when(jnp.logical_and(alone, jnp.logical_not(has_far)))(
                    lambda: update(False, False)
                )
            else:
                pl.when(has_far)(lambda: update(True, False))
                pl.when(jnp.logical_not(has_far))(lambda: update(False, False))
            if send:
                send_piece(t + 1, c, piece)

    def steps(t, c):
        return [
            lambda: add(t, c, E),
            lambda: add(t, c, B, wait=True),
            lambda: add(t, c, D, wait=True),
            lambda: add_faces(t, c),
        ]

    def sweep(t):
        first = t == 0
        last = t == ITERS - 1
        more = not last
        straight = lax.rem(e, 2) == 0 if last else None

        def opening():
            gather(0, 0)
            send_own(0, 1, (A,))

        def earlier():
            before = steps(t - 1, 1)
            before[0]()
            gather(t, 0, [lambda: send_traces(t, 0)] + before[1:2] + before[3:4])
            finish(t - 1, 1, True)

        opening() if first else earlier()

        if first:
            for index in range(BAND):
                jac_loads[index].wait()
            for load in lift_loads:
                load.wait()

        pass_on(t, 0, [lambda: begin(t, 0), lambda: add(t, 0, A), lambda: add(t, 0, C)])
        send_late(t, 1)
        middle = steps(t, 0)
        middle[0]()
        gather(t, 1, [lambda: send_traces(t, 1)] + middle[1:2] + middle[3:4], straight)
        if more:
            finish(t, 0, True)
        pass_on(
            t, 1, [lambda: begin(t, 1), lambda: add(t, 1, A), lambda: add(t, 1, C)], straight
        )
        if more:
            send_late(t + 1, 0)

    for t in range(ITERS):
        sweep(t)
    add(ITERS - 1, 0, D, wait=True)
    finish(ITERS - 1, 0, None)
    for task in steps(ITERS - 1, 1):
        task()
    for kind, condition in sending.items():

        def wait(kind=kind):
            pltpu.make_async_remote_copy(
                src_ref=slots.at[kind],
                dst_ref=slots.at[kind],
                send_sem=send_sem.at[kind],
                recv_sem=recv_sem.at[0, 0, 0],
                device_id={"harm": partner},
                device_id_type=pl.DeviceIdType.MESH,
            ).wait_send()

        guarded(condition, wait)
    for place, kind, target in ((0, LOWER, below), (1, UPPER, above)):
        pltpu.make_async_remote_copy(
            src_ref=traces.at[place],
            dst_ref=faces.at[place],
            send_sem=send_sem.at[kind],
            recv_sem=recv_sem.at[0, 0, kind],
            device_id={"ax": target},
            device_id_type=pl.DeviceIdType.MESH,
        ).wait_send()
    finish(ITERS - 1, 1, None)


def local(forcing, jacobian, lift_lower, lift_upper, orient):
    rows, columns = forcing.shape[2:]
    width = columns // PARTS
    bf16 = jnp.bfloat16
    any_space = pl.BlockSpec(memory_space=pl.ANY)
    return pl.pallas_call(
        functools.partial(kernel, lax.axis_size("harm"), lax.axis_size("ax"), width),
        out_shape=pltpu.VMEM(forcing.shape, bf16),
        in_specs=[pl.BlockSpec(memory_space=pltpu.SMEM)] + [any_space] * 4,
        out_specs=pl.BlockSpec(memory_space=pltpu.VMEM),
        scratch_shapes=[
            pltpu.VMEM((BAND, rows, rows), bf16),
            pltpu.VMEM(lift_lower.shape, bf16),
            pltpu.VMEM(lift_upper.shape, bf16),
            pltpu.VMEM((ITERS + 1, PARTS, rows, width), bf16),
            pltpu.VMEM((6, ITERS, PARTS, rows, width), bf16),
            pltpu.VMEM((2, ITERS, PARTS, FPAD, width), bf16),
            pltpu.VMEM((2, ITERS, PARTS, FPAD, width), bf16),
            pltpu.VMEM((2, FPAD, rows), bf16),
            pltpu.VMEM((PARTS, rows, width), jnp.float32),
            pltpu.SemaphoreType.DMA((PARTS + 2,)),
            pltpu.SemaphoreType.DMA((BAND,)),
            pltpu.SemaphoreType.DMA((KINDS,)),
            pltpu.SemaphoreType.DMA((ITERS, PARTS, len(RELAYED), PIECES)),
            pltpu.SemaphoreType.DMA((ITERS, PARTS, KINDS)),
        ],
        compiler_params=pltpu.CompilerParams(collective_id=0, has_side_effects=True),
        name="sweeps",
    )(orient, forcing, jacobian, lift_lower, lift_upper)


def solution(mesh):
    placed = (P("harm", "ax", None, None), P("harm", None, "ax", None, None), P(), P(), P())
    return jax.shard_map(
        local, mesh=mesh, in_specs=placed, out_specs=P("harm", "ax", None, None), check_vma=False
    )
```

```python
import functools

import jax
import jax.numpy as jnp
from jax import lax
from jax.experimental import pallas as pl
from jax.experimental.pallas import tpu as pltpu
from jax.sharding import PartitionSpec as P

NVAR = 5
ND = 5
BAND = 7
ITERS = 3
FN = 125
NF = ND * ND
NP = NVAR * ND * NF
FPAD = 128
PARTS = 2

relaxation = 0.5

A, B, C, D, E, F = range(6)
OFFSETS = (1, -2, 2, 3, -1, -3)
LOWER, UPPER = 6, 7
KINDS = 8
RELAYED = {A: 0, C: 1, E: 2}
PIECES = 4
DIRECT = (3,)
ROW_TILE = 16


def divided(value, by):
    factor, shift = {5: (13108, 16), 25: (2622, 16), 125: (1049, 17)}[by]
    return lax.shift_right_logical(value * factor, shift)


def mapped(node, orient_value):
    swap = lax.rem(lax.div(orient_value, 4), 2)
    flip_b = lax.rem(orient_value, 2)
    flip_c = lax.rem(lax.div(orient_value, 2), 2)
    first = divided(node, ND)
    second = node - first * ND
    first_a = first + swap * (second - first)
    second_a = second + swap * (first - second)
    first_b = first_a + flip_b * (ND - 1 - 2 * first_a)
    second_b = second_a + flip_c * (ND - 1 - 2 * second_a)
    return first_b * ND + second_b


def kernel(
    harm_count, ax_count, width,
    orient_ref, forcing_ref, jac_ref, lower_ref, upper_ref, out_ref,
    jac, lift_lo, lift_up, own, slots, traces, faces, pick, acc,
    load_sem, jac_sem, send_sem, relay_sem, recv_sem,
):
    h = lax.axis_index("harm")
    e = lax.axis_index("ax")
    s = 1 - 2 * lax.rem(h, 2)
    reach = BAND // 2
    partner = h + s
    ahead = h + 2 * s
    behind = h - 2 * s
    has_ahead = jnp.logical_and(ahead >= 0, ahead < harm_count)
    has_behind = jnp.logical_and(behind >= 0, behind < harm_count)
    far = h - 3 * s
    has_far = jnp.logical_and(far >= 0, far < harm_count)
    has_both = jnp.logical_and(has_ahead, has_behind)
    above = lax.rem(e + 1, ax_count)
    below = lax.rem(e + ax_count - 1, ax_count)

    barrier = pltpu.get_barrier_semaphore()

    across = h - s
    has_across = jnp.logical_and(across >= 0, across < harm_count)

    def greet(axis, index):
        pl.semaphore_signal(
            barrier, inc=1, device_id={axis: index}, device_id_type=pl.DeviceIdType.MESH
        )

    greet("harm", partner)
    greet("ax", above)
    greet("ax", below)

    @pl.when(has_ahead)
    def _():
        greet("harm", ahead)

    @pl.when(has_behind)
    def _():
        greet("harm", behind)

    @pl.when(has_across)
    def _():
        greet("harm", across)

    loads = [
        pltpu.make_async_copy(
            forcing_ref.at[0, 0, :, pl.ds(c * width, width)], own.at[0, c], load_sem.at[c]
        )
        for c in range(PARTS)
    ]
    for load in loads:
        load.start()
    jac_loads = [
        pltpu.make_async_copy(jac_ref.at[0, reach + k * s, 0], jac.at[i], jac_sem.at[i])
        for i, k in enumerate(OFFSETS + (0,))
    ]
    lift_loads = [
        pltpu.make_async_copy(lower_ref, lift_lo, load_sem.at[PARTS]),
        pltpu.make_async_copy(upper_ref, lift_up, load_sem.at[PARTS + 1]),
    ]

    pl.semaphore_wait(
        barrier,
        3
        + has_ahead.astype(jnp.int32)
        + has_behind.astype(jnp.int32)
        + has_across.astype(jnp.int32),
    )

    rows = own.shape[2]
    step = -(-rows // (PIECES * ROW_TILE)) * ROW_TILE
    cuts = [(start, min(step, rows - start)) for start in range(0, rows, step)]

    def transfer(t, c, kind, piece, direct=False):
        mine = own.at[t, c]
        source, target = {
            A: (mine, partner),
            B: (mine, ahead),
            C: (mine, behind),
            D: (slots.at[A, t, c], behind),
            E: (slots.at[C, t, c], partner),
            F: (slots.at[C, t, c], across) if direct else (slots.at[E, t, c], ahead),
        }[kind]
        part = slice(None) if piece is None else pl.ds(*cuts[piece])
        return pltpu.make_async_remote_copy(
            src_ref=source.at[part],
            dst_ref=slots.at[kind, t, c, part],
            send_sem=send_sem.at[kind],
            recv_sem=relay_sem.at[t, c, RELAYED[kind], piece]
            if kind in RELAYED
            else recv_sem.at[t, c, kind],
            device_id={"harm": target},
            device_id_type=pl.DeviceIdType.MESH,
        )

    sending = {
        A: None, B: has_ahead, C: has_behind, D: has_behind, E: has_ahead, F: has_both
    }
    getting = {
        A: None, B: has_behind, C: has_ahead, D: has_ahead, E: has_behind, F: has_far
    }

    def guarded(condition, action):
        if condition is None:
            action()
        else:
            pl.when(condition)(action)

    def face_transfers(t, c):
        result = []
        for place, kind, target in ((0, LOWER, below), (1, UPPER, above)):
            result.append(
                pltpu.make_async_remote_copy(
                    src_ref=traces.at[place, t, c],
                    dst_ref=faces.at[place, t, c],
                    send_sem=send_sem.at[kind],
                    recv_sem=recv_sem.at[t, c, kind],
                    device_id={"ax": target},
                    device_id_type=pl.DeviceIdType.MESH,
                )
            )
        return result

    def send_own(t, c, kinds):
        for piece in range(len(cuts)):
            send_piece(t, c, piece, kinds)

    def send_piece(t, c, piece, kinds=(C, A)):
        for kind in kinds:
            guarded(sending[kind], lambda: transfer(t, c, kind, piece).start())

    def send_late(t, c):
        guarded(sending[B], lambda: transfer(t, c, B, None).start())

    def send_traces(t, c):
        for place in range(2):
            traces[place, t, c] = jnp.dot(
                pick[place], own[t, c], preferred_element_type=jnp.float32
            ).astype(jnp.bfloat16)
        for copy in face_transfers(t, c):
            copy.start()

    def add(t, c, kind, wait=False):
        def action():
            if wait:
                transfer(t, c, kind, None).wait_recv()
            acc[c] += jnp.dot(jac[kind], slots[kind, t, c], preferred_element_type=jnp.float32)

        guarded(getting[kind], action)

    def begin(t, c):
        acc[c] = jnp.dot(jac[BAND - 1], own[t, c], preferred_element_type=jnp.float32)

    loads[0].wait()
    send_own(0, 0, (C, A))
    send_late(0, 0)
    loads[1].wait()
    send_own(0, 1, (C,))
    for i in (BAND - 1, A, C, B, E, D, F):
        jac_loads[i].start()
    for load in lift_loads:
        load.start()

    row = lax.broadcasted_iota(jnp.int32, (FPAD, NP), 0)
    column = lax.broadcasted_iota(jnp.int32, (FPAD, NP), 1)
    row_variable = divided(row, NF)
    row_node = row - row_variable * NF
    column_variable = divided(column, FN)
    column_node = column - column_variable * FN
    low_target = row_variable * FN + mapped(row_node, orient_ref[below])
    pick[0] = jnp.where(column == low_target, 1.0, 0.0).astype(jnp.bfloat16)
    up_node = column_node - (ND - 1) * NF
    up_image = mapped(jnp.maximum(up_node, 0), orient_ref[e])
    up_row = jnp.where(up_node >= 0, column_variable * NF + up_image, -1)
    pick[1] = jnp.where(up_row == row, 1.0, 0.0).astype(jnp.bfloat16)

    send_traces(0, 0)

    def gather(t, c, tasks=(), straight=None):
        tasks = list(tasks)
        count = len(cuts)
        for piece in range(count):

            def from_ahead(piece=piece):
                transfer(t, c, C, piece).wait_recv()
                if straight is not None and piece in DIRECT:
                    pl.when(jnp.logical_and(straight, has_across))(
                        lambda: transfer(t, c, F, piece, True).start()
                    )
                transfer(t, c, E, piece).start()

            pl.when(has_ahead)(from_ahead)
            transfer(t, c, A, piece).wait_recv()
            pl.when(has_behind)(lambda: transfer(t, c, D, piece).start())
            for task in tasks[piece : piece + 1] if piece < count - 1 else tasks[piece:]:
                task()

    def pass_on(t, c, tasks=(), straight=None):
        tasks = list(tasks)
        count = len(cuts)
        for piece in range(count):

            def onward(piece=piece):
                transfer(t, c, E, piece).wait_recv()
                onward_too = has_ahead
                if straight is not None and piece in DIRECT:
                    onward_too = jnp.logical_and(has_ahead, jnp.logical_not(straight))
                pl.when(onward_too)(lambda: transfer(t, c, F, piece).start())

            pl.when(has_behind)(onward)
            for task in tasks[piece : piece + 1] if piece < count - 1 else tasks[piece:]:
                task()

    def add_faces(t, c):
        for copy in face_transfers(t, c):
            copy.wait_recv()
        acc[c] += jnp.dot(
            lift_up[...], faces[0, t, c, :FN], preferred_element_type=jnp.float32
        ) + jnp.dot(lift_lo[...], faces[1, t, c, :FN], preferred_element_type=jnp.float32)

    def finish(t, c, send):
        merged = send is not None
        if merged:
            guarded(getting[D], lambda: transfer(t, c, D, None).wait_recv())
        guarded(getting[F], lambda: transfer(t, c, F, None).wait_recv())
        for piece, (start, size) in enumerate(cuts):
            part = slice(start, start + size)

            def update(last_term, far_term):
                total = acc[c, part]
                if far_term:
                    total = total + jnp.dot(
                        jac[D, part], slots[D, t, c], preferred_element_type=jnp.float32
                    )
                if last_term:
                    total = total + jnp.dot(
                        jac[F, part], slots[F, t, c], preferred_element_type=jnp.float32
                    )
                updated = own[t, c, part].astype(jnp.float32) + relaxation * (
                    own[0, c, part].astype(jnp.float32) - total
                )
                updated = updated.astype(jnp.bfloat16)
                if send is None:
                    out_ref[0, 0, part, c * width : (c + 1) * width] = updated
                else:
                    own[t + 1, c, part] = updated

            if merged:
                short = jnp.logical_and(has_ahead, jnp.logical_not(has_far))
                pl.when(jnp.logical_and(has_ahead, has_far))(lambda: update(True, True))
                pl.when(short)(lambda: update(False, True))
                alone = jnp.logical_not(has_ahead)
                pl.when(jnp.logical_and(alone, has_far))(lambda: update(True, False))
                pl.when(jnp.logical_and(alone, jnp.logical_not(has_far)))(
                    lambda: update(False, False)
                )
            else:
                pl.when(has_far)(lambda: update(True, False))
                pl.when(jnp.logical_not(has_far))(lambda: update(False, False))
            if send:
                send_piece(t + 1, c, piece)

    def steps(t, c):
        return [
            lambda: add(t, c, E),
            lambda: add(t, c, B, wait=True),
            lambda: add(t, c, D, wait=True),
            lambda: add_faces(t, c),
        ]

    def sweep(t):
        first = t == 0
        last = t == ITERS - 1
        more = not last
        straight = lax.rem(e, 2) == 0 if last else None

        def opening():
            gather(0, 0)
            send_own(0, 1, (A,))

        def earlier():
            before = steps(t - 1, 1)
            before[0]()
            gather(t, 0, [lambda: send_traces(t, 0)] + before[1:2] + before[3:4])
            finish(t - 1, 1, True)

        opening() if first else earlier()

        if first:
            for index in range(BAND):
                jac_loads[index].wait()
            for load in lift_loads:
                load.wait()

        pass_on(t, 0, [lambda: begin(t, 0), lambda: add(t, 0, A), lambda: add(t, 0, C)])
        send_late(t, 1)
        middle = steps(t, 0)
        middle[0]()
        gather(t, 1, [lambda: send_traces(t, 1)] + middle[1:2] + middle[3:4], straight)
        if more:
            finish(t, 0, True)
        closing = [lambda: begin(t, 1), lambda: add(t, 1, A), lambda: add(t, 1, C)]
        if last:
            closing[1:] = [
                lambda: (add(t, 1, A), add(t, 1, C)),
                lambda: (add(t, 0, D, wait=True), finish(t, 0, None)),
            ]
        pass_on(t, 1, closing, straight)
        if more:
            send_late(t + 1, 0)

    for t in range(ITERS):
        sweep(t)
    for task in steps(ITERS - 1, 1):
        task()
    for kind, condition in sending.items():

        def wait(kind=kind):
            pltpu.make_async_remote_copy(
                src_ref=slots.at[kind],
                dst_ref=slots.at[kind],
                send_sem=send_sem.at[kind],
                recv_sem=recv_sem.at[0, 0, 0],
                device_id={"harm": partner},
                device_id_type=pl.DeviceIdType.MESH,
            ).wait_send()

        guarded(condition, wait)
    for place, kind, target in ((0, LOWER, below), (1, UPPER, above)):
        pltpu.make_async_remote_copy(
            src_ref=traces.at[place],
            dst_ref=faces.at[place],
            send_sem=send_sem.at[kind],
            recv_sem=recv_sem.at[0, 0, kind],
            device_id={"ax": target},
            device_id_type=pl.DeviceIdType.MESH,
        ).wait_send()
    finish(ITERS - 1, 1, None)


def local(forcing, jacobian, lift_lower, lift_upper, orient):
    rows, columns = forcing.shape[2:]
    width = columns // PARTS
    bf16 = jnp.bfloat16
    any_space = pl.BlockSpec(memory_space=pl.ANY)
    return pl.pallas_call(
        functools.partial(kernel, lax.axis_size("harm"), lax.axis_size("ax"), width),
        out_shape=pltpu.VMEM(forcing.shape, bf16),
        in_specs=[pl.BlockSpec(memory_space=pltpu.SMEM)] + [any_space] * 4,
        out_specs=pl.BlockSpec(memory_space=pltpu.VMEM),
        scratch_shapes=[
            pltpu.VMEM((BAND, rows, rows), bf16),
            pltpu.VMEM(lift_lower.shape, bf16),
            pltpu.VMEM(lift_upper.shape, bf16),
            pltpu.VMEM((ITERS + 1, PARTS, rows, width), bf16),
            pltpu.VMEM((6, ITERS, PARTS, rows, width), bf16),
            pltpu.VMEM((2, ITERS, PARTS, FPAD, width), bf16),
            pltpu.VMEM((2, ITERS, PARTS, FPAD, width), bf16),
            pltpu.VMEM((2, FPAD, rows), bf16),
            pltpu.VMEM((PARTS, rows, width), jnp.float32),
            pltpu.SemaphoreType.DMA((PARTS + 2,)),
            pltpu.SemaphoreType.DMA((BAND,)),
            pltpu.SemaphoreType.DMA((KINDS,)),
            pltpu.SemaphoreType.DMA((ITERS, PARTS, len(RELAYED), PIECES)),
            pltpu.SemaphoreType.DMA((ITERS, PARTS, KINDS)),
        ],
        compiler_params=pltpu.CompilerParams(collective_id=0, has_side_effects=True),
        name="sweeps",
    )(orient, forcing, jacobian, lift_lower, lift_upper)


def solution(mesh):
    placed = (P("harm", "ax", None, None), P("harm", None, "ax", None, None), P(), P(), P())
    return jax.shard_map(
        local, mesh=mesh, in_specs=placed, out_specs=P("harm", "ax", None, None), check_vma=False
    )
```
